256 devices in a mesh: seq: 32 (over z, x), head: 8 (over y, core).
Axes of the slice: x: 4, y: 4, z: 8, core: 2. Of those that a mesh axis runs over, the one named last changes fastest.
Arguments:
- queries: bfloat16 [8192, 8192], P('seq', 'head'), may hold values from -6 to 6
- key_rows: bfloat16 [8192, 8192], P('seq', 'head'), may hold values from -6 to 6
- value_rows: bfloat16 [8192, 8192], P('seq', 'head'), may hold values from -160 to 160
- log_decay: float32 [8192, 64], P('seq', 'head'), may hold values from -0.5 to 0, as said below
- gate_input: bfloat16 [8192, 8192], P('seq', 'head'), may hold values from -12 to 12
- out_gain: float32 [8192], P('head'), may hold values from 0.1 to 1.9
- prior_state: float32 [64, 128, 128], P('head'), may hold values from -192 to 192
- out_grad: bfloat16 [8192, 8192], P('seq', 'head'), may hold values from -6 to 6
Outputs:
- attended: bfloat16 [8192, 8192], P('seq', 'head')
- grad_query: bfloat16 [8192, 8192], P('seq', 'head')
- grad_key: bfloat16 [8192, 8192], P('seq', 'head')
- grad_value: bfloat16 [8192, 8192], P('seq', 'head')
- grad_gate: bfloat16 [8192, 8192], P('seq', 'head')
The draws below stay inside these ranges and needn't reach their ends.
Inputs may be any that keep to these rules, and one draw needn't show every extreme that they name: `log_decay`: every entry is negative; at each token a head's state is multiplied by exp(entry).
All inputs are finite; a program needn't handle non-finite values.
Results may differ from the reference program's by a relative error of at most 0.012.
Values sent between devices are 32-bit elements; how exact they have to be, the bound alone decides.
No kernel may reach another device: no remote copies, remote signals or barrier semaphores. Data moves between devices by JAX's collectives and lax.ppermute only.
A program may use at most 64 MiB of HBM per device.

```python
import math
import jax
import jax.numpy as jnp
from jax import lax

HEAD_TOTAL = 64
HD = 128
BLK = 256
D = 8192
WINDOW_TOKENS = 8192


def draw_log_decay(key, part):
    pick_key, slow_key, fast_key, rough_key, location_key, falloff_key = jax.random.split(key, 6)
    pick_draw = jax.random.randint(pick_key, (HEAD_TOTAL,), 0, 10)
    is_slow = pick_draw < 5
    slow_rate = jnp.exp(jax.random.uniform(slow_key, (HEAD_TOTAL,), jnp.float32, math.log(4e-06), math.log(4e-05)))
    fast_rate = jnp.exp(jax.random.uniform(fast_key, (HEAD_TOTAL,), jnp.float32, math.log(0.02), math.log(0.033)))
    decay_speed = jnp.where(is_slow, slow_rate, fast_rate)
    jaggedness = jax.random.uniform(rough_key, (WINDOW_TOKENS, HEAD_TOTAL), jnp.float32, 0.5, 1.5)
    spike_position = jax.random.randint(location_key, (3,), 0, WINDOW_TOKENS)
    spike_row = jnp.any(jnp.arange(WINDOW_TOKENS)[:, None] == spike_position[None, :], axis=1)
    spike_falloff = jax.random.uniform(falloff_key, (WINDOW_TOKENS, HEAD_TOTAL), jnp.float32, 0.22, 0.5)
    return jnp.where(spike_row[:, None], -spike_falloff, -decay_speed[None, :] * jaggedness).astype(jnp.float32)


def draw_value_rows(key, part):
    ramp_key = jax.random.fold_in(key, 0)
    base_key = jax.random.fold_in(key, 1)
    row_key = jax.random.fold_in(key, 3)
    head_place = (jnp.arange(D) // HD).astype(jnp.float32) / (HEAD_TOTAL - 1)
    column_scale = jnp.exp(math.log(3.0) * head_place + jax.random.uniform(ramp_key, (D,), jnp.float32, 0.0, math.log(10.0 / 3.0)))
    base_draw = jnp.clip(jax.random.normal(base_key, (WINDOW_TOKENS, D), jnp.float32), -4.0, 4.0)
    row_scale = jnp.exp(jax.random.uniform(row_key, (WINDOW_TOKENS, 1), jnp.float32, 0.0, math.log(4.0)))
    return (base_draw * column_scale[None, :] * row_scale).astype(jnp.bfloat16)


def shard_levels(rng, extent, cuts, low, high):
    loudness = 1.0
    for dim, shards_of in cuts:
        draws = jax.random.uniform(jax.random.fold_in(jax.random.fold_in(rng, 6), dim), (shards_of,), jnp.float32, low / len(cuts), high / len(cuts))
        loudness = loudness * jnp.repeat(jnp.exp(draws), extent[dim] // shards_of).reshape((-1,) + (1,) * (len(extent) - 1 - dim))
    return loudness


def scatter_about(stream_key, extent, scale, limit, cuts=(), dtype=jnp.bfloat16):
    array = jax.random.normal(stream_key, extent, jnp.float32) * scale
    if len(cuts) > 0:
        array = shard_levels(stream_key, extent, cuts, -0.22, 0.18) * array
    return jnp.clip(array, min=-limit, max=limit).astype(dtype)


def setup_inputs(seed: int = 0) -> dict:
    splits = jax.random.split(jax.random.key(seed), 9)
    return {
        "queries": scatter_about(splits[0], (WINDOW_TOKENS, D), 1.0, 6.0, ((0, 32), (1, 8))),
        "key_rows": scatter_about(splits[1], (WINDOW_TOKENS, D), 1.0, 6.0, ((0, 32), (1, 8))),
        "value_rows": draw_value_rows(jax.random.fold_in(splits[8], 71), 0),
        "log_decay": draw_log_decay(jax.random.fold_in(splits[8], 71), 0),
        "gate_input": scatter_about(splits[4], (WINDOW_TOKENS, D), 2.0, 12.0, ((0, 32), (1, 8))),
        "out_gain": jnp.clip(1.0 + 0.18 * jax.random.normal(splits[5], (D,), jnp.float32), 0.1, 1.9),
        "prior_state": scatter_about(splits[6], (HEAD_TOTAL, HD, HD), 32.0, 192.0, ((0, 8),), jnp.float32),
        "out_grad": scatter_about(splits[7], (WINDOW_TOKENS, D), 1.0, 6.0, ((0, 32), (1, 8))),
    }


epsilon = 1e-06
highest = lax.Precision.HIGHEST

def decay_tables(decay_block):
    running = jnp.cumsum(decay_block, axis=0)
    closing = running[-1]
    spread = running.T[:, :, None] - running.T[:, None, :]
    causal = jnp.arange(decay_block.shape[0])[:, None] >= jnp.arange(decay_block.shape[0])[None, :]
    weights = jnp.where(causal[None], jnp.exp(jnp.minimum(spread, 0.0)), 0.0)
    return (running, closing, weights)

def mixing_of(query_wide, key_wide, weights):
    scores = jnp.einsum('the,she->hts', query_wide, key_wide, precision=highest)
    mixing = (scores * weights).astype(jnp.bfloat16)
    return lax.optimization_barrier(mixing).astype(jnp.float32)

def forward_step(carried, inputs):
    query_block, key_block, value_block, decay_block = inputs
    running, closing, weights = decay_tables(decay_block)
    query_wide = query_block.astype(jnp.float32)
    key_wide = key_block.astype(jnp.float32)
    value_wide = value_block.astype(jnp.float32)
    mixing = mixing_of(query_wide, key_wide, weights)
    within = jnp.einsum('hts,she->the', mixing, value_wide, precision=highest)
    across = jnp.exp(running)[:, :, None] * jnp.einsum('the,hef->thf', query_wide, carried, precision=highest)
    remain = jnp.exp(closing[None, :] - running)
    updated = jnp.exp(closing)[:, None, None] * carried + jnp.einsum('she,shf->hef', key_wide * remain[:, :, None], value_wide, precision=highest)
    return (updated, (within + across, carried))

def backward_step(returned, inputs):
    query_block, key_block, value_block, grad_rows, decay_block, opening = inputs
    running, closing, weights = decay_tables(decay_block)
    query_wide = query_block.astype(jnp.float32)
    key_wide = key_block.astype(jnp.float32)
    value_wide = value_block.astype(jnp.float32)
    grad_wide = grad_rows.astype(jnp.float32)
    mixing = mixing_of(query_wide, key_wide, weights)
    grad_scores = jnp.einsum('thf,shf->hts', grad_wide, value_wide, precision=highest)
    grad_mixing = lax.optimization_barrier((grad_scores * weights).astype(jnp.bfloat16)).astype(jnp.float32)
    grad_q = jnp.einsum('hts,she->the', grad_mixing, key_wide, precision=highest) + jnp.exp(running)[:, :, None] * jnp.einsum('thf,hef->the', grad_wide, opening, precision=highest)
    remain = jnp.exp(closing[None, :] - running)[:, :, None]
    grad_k = jnp.einsum('hts,the->she', grad_mixing, query_wide, precision=highest) + remain * jnp.einsum('shf,hef->she', value_wide, returned, precision=highest)
    grad_v = jnp.einsum('hts,thf->shf', mixing, grad_wide, precision=highest) + remain * jnp.einsum('she,hef->shf', key_wide, returned, precision=highest)
    summed = jnp.einsum('the,thf->hef', query_wide * jnp.exp(running)[:, :, None], grad_wide, precision=highest)
    updated = summed + jnp.exp(closing)[:, None, None] * returned
    return (updated, (grad_q, grad_k, grad_v))

def reference(queries, key_rows, value_rows, log_decay, gate_input, out_gain, prior_state, out_grad):
    blocks = WINDOW_TOKENS // BLK
    block_shape = (blocks, BLK, HEAD_TOTAL, HD)
    query_all = queries.reshape(block_shape)
    key_all = key_rows.reshape(block_shape)
    value_all = value_rows.reshape(block_shape)
    decay_all = log_decay.reshape(blocks, BLK, HEAD_TOTAL)
    final_state, (context_parts, openings) = lax.scan(forward_step, prior_state.astype(jnp.float32), (query_all, key_all, value_all, decay_all))
    merged = context_parts.reshape(WINDOW_TOKENS, D)
    inverse = lax.rsqrt(lax.optimization_barrier(jnp.sum(merged * merged, axis=1)) / D + epsilon)
    normed = merged * inverse[:, None]
    opened = jax.nn.sigmoid(gate_input.astype(jnp.float32))
    attended = (normed * out_gain * opened).astype(jnp.bfloat16)
    grad_wide = out_grad.astype(jnp.float32)
    grad_gate = (grad_wide * normed * out_gain * opened * (1.0 - opened)).astype(jnp.bfloat16)
    grad_norm = grad_wide * out_gain * opened
    row_dot = lax.optimization_barrier(jnp.sum(merged * grad_norm, axis=1))
    grad_merged = inverse[:, None] * grad_norm - merged * (inverse * inverse * inverse * row_dot / D)[:, None]
    grad_context = grad_merged.astype(jnp.bfloat16)
    grad_all = grad_context.reshape(block_shape)
    zero_state = jnp.zeros((HEAD_TOTAL, HD, HD), jnp.float32)
    unused, (grad_q_parts, grad_k_parts, grad_v_parts) = lax.scan(backward_step, zero_state, (query_all, key_all, value_all, grad_all, decay_all, openings), reverse=True)
    grad_query = grad_q_parts.reshape(WINDOW_TOKENS, D).astype(jnp.bfloat16)
    grad_key = grad_k_parts.reshape(WINDOW_TOKENS, D).astype(jnp.bfloat16)
    grad_value = grad_v_parts.reshape(WINDOW_TOKENS, D).astype(jnp.bfloat16)
    return (attended, grad_query, grad_key, grad_value, grad_gate)
```

```python
import jax
import jax.numpy as jnp
from jax import lax
from jax.experimental import pallas as pl
from jax.experimental.pallas import tpu as pltpu
from jax.sharding import PartitionSpec as P

D = 8192
HD = 128
epsilon = 1e-06

F32 = jnp.float32
BF16 = jnp.bfloat16
MIB = 1 << 20


def dot(left, right, dims, precision=None):
    return lax.dot_general(
        left, right, (dims, ((), ())), precision=precision, preferred_element_type=F32
    )


NN = ((1,), (0,))
NT = ((1,), (1,))
TN = ((0,), (0,))


def cols(h):
    return slice(h * HD, (h + 1) * HD)


def exact_sum(table, decay):
    return dot(table.astype(F32), decay, NN, lax.Precision.HIGHEST)


def square_iota(n):
    row = lax.broadcasted_iota(jnp.int32, (n, n), 0)
    col = lax.broadcasted_iota(jnp.int32, (n, n), 1)
    return row, col


def state_kernel(k_ref, v_ref, decay_ref, out_ref, remain_ref):
    tokens, heads = decay_ref.shape
    row, col = square_iota(tokens)
    decay = decay_ref[...]
    remain = jnp.exp(exact_sum(col > row, decay))
    remain_ref[...] = remain
    closing = jnp.sum(decay, axis=0, keepdims=True)
    slices = out_ref.shape[0] // heads
    rows = HD // slices
    for h in range(heads):
        scaled = (v_ref[:, cols(h)].astype(F32) * remain[:, h : h + 1]).astype(BF16)
        state = dot(k_ref[:, cols(h)], scaled, TN)
        last = jnp.broadcast_to(closing[:, h : h + 1], (8, HD))
        for i in range(slices):
            out_ref[h * slices + i, 0:rows, :] = state[i * rows : (i + 1) * rows]
            out_ref[h * slices + i, rows : rows + 8, :] = last


def forward_chain_kernel(parts_ref, prior_ref, out_ref, factor_ref):
    count, rows, _ = out_ref.shape
    carried = prior_ref[0]
    for d in range(count):
        out_ref[d] = carried
        factor = jnp.exp(parts_ref[d, rows : rows + 8, :])
        factor_ref[d] = factor
        carried = factor[0:1] * carried + parts_ref[d, 0:rows, :]


def backward_chain_kernel(parts_ref, factor_ref, out_ref):
    count = out_ref.shape[0]
    returned = jnp.zeros(out_ref.shape[1:], F32)
    for d in range(count - 1, -1, -1):
        out_ref[d] = returned
        returned = factor_ref[d, 0:1, :] * returned + parts_ref[d]


def head_weights(running, running_rows, h, causal):
    spread = running[:, h : h + 1] - running_rows[h : h + 1, :]
    return jnp.where(causal, jnp.exp(jnp.minimum(spread, 0.0)), 0.0)


def within_kernel(
    q_ref, k_ref, v_ref, decay_ref, gate_ref, grad_ref, gain_ref,
    within_ref, mixing_ref, norm_grad_ref, grown_ref,
):
    tokens, heads = decay_ref.shape
    row, col = square_iota(tokens)
    causal = row >= col
    decay = decay_ref[...]
    running = exact_sum(causal, decay)
    running_rows = dot(decay, causal.astype(F32), ((0,), (1,)), lax.Precision.HIGHEST)
    grown_ref[...] = jnp.exp(running)
    for h in range(heads):
        c = cols(h)
        scores = dot(q_ref[:, c], k_ref[:, c], NT)
        mixing = (scores * head_weights(running, running_rows, h, causal)).astype(BF16)
        mixing_ref[h] = mixing
        within_ref[:, c] = dot(mixing, v_ref[:, c], NN)
        opened = jax.nn.sigmoid(gate_ref[:, c].astype(F32))
        norm_grad_ref[:, c] = grad_ref[:, c].astype(F32) * gain_ref[:, c] * opened


def context_kernel(
    q_ref, within_ref, norm_grad_ref, grown_ref, state_ref, context_ref, sums_ref
):
    tokens, heads = grown_ref.shape
    slices = state_ref.shape[0] // heads
    grown = grown_ref[...]
    squares = jnp.zeros((tokens, HD), F32)
    products = jnp.zeros((tokens, HD), F32)
    for h in range(heads):
        c = cols(h)
        state = state_ref[h * slices : (h + 1) * slices].reshape(HD, HD).astype(BF16)
        context = within_ref[:, c] + grown[:, h : h + 1] * dot(q_ref[:, c], state, NN)
        context_ref[:, c] = context
        squares += context * context
        products += context * norm_grad_ref[:, c]
    ones = jnp.ones((8, HD), F32)
    square_rows = dot(ones, squares, NT, lax.Precision.HIGHEST)
    product_rows = dot(ones, products, NT, lax.Precision.HIGHEST)
    first = lax.broadcasted_iota(jnp.int32, square_rows.shape, 0) == 0
    both = jnp.where(first, square_rows, product_rows)
    for p in range(sums_ref.shape[0]):
        sums_ref[p] = both


def gradient_kernel(
    sums_ref, q_ref, context_ref, norm_grad_ref, grown_ref, grad_ref, out_ref, inverse_ref
):
    tokens, heads = grown_ref.shape
    total = sums_ref[0]
    for p in range(1, sums_ref.shape[0]):
        total = total + sums_ref[p]
    pick = lax.broadcasted_iota(jnp.int32, (8, HD), 0)
    square = dot(total, (pick == 0).astype(F32), TN, lax.Precision.HIGHEST)
    product = dot(total, (pick == 1).astype(F32), TN, lax.Precision.HIGHEST)
    inverse = lax.rsqrt(square / D + epsilon)
    inverse_ref[...] = inverse
    slope = inverse * inverse * inverse * product / D
    grown = grown_ref[...]
    slices = out_ref.shape[0] // heads
    rows = HD // slices
    for h in range(heads):
        c = cols(h)
        grad = (inverse * norm_grad_ref[:, c] - context_ref[:, c] * slope).astype(BF16)
        grad_ref[:, c] = grad
        scaled = (q_ref[:, c].astype(F32) * grown[:, h : h + 1]).astype(BF16)
        state = dot(scaled, grad, TN)
        for i in range(slices):
            out_ref[h * slices + i] = state[i * rows : (i + 1) * rows]


def local_backward_kernel(
    q_ref, k_ref, v_ref, grad_ref, state_ref, mixing_ref, decay_ref, grown_ref,
    gate_ref, norm_grad_ref, context_ref, gain_ref, inverse_ref,
    attended_ref, grad_gate_ref, grad_q_ref, grad_k_ref, grad_v_ref,
):
    tokens, heads = decay_ref.shape
    row, col = square_iota(tokens)
    causal = row >= col
    decay = decay_ref[...]
    running = exact_sum(causal, decay)
    running_rows = dot(decay, causal.astype(F32), ((0,), (1,)), lax.Precision.HIGHEST)
    grown = grown_ref[...]
    inverse = inverse_ref[...]
    slices = state_ref.shape[0] // heads
    for h in range(heads):
        c = cols(h)
        opened = jax.nn.sigmoid(gate_ref[:, c].astype(F32))
        normed = context_ref[:, c] * inverse
        attended_ref[:, c] = (normed * gain_ref[:, c] * opened).astype(BF16)
        grad_gate_ref[:, c] = (norm_grad_ref[:, c] * normed * (1.0 - opened)).astype(BF16)
        grad = grad_ref[:, c]
        scores = dot(grad, v_ref[:, c], NT)
        weights = head_weights(running, running_rows, h, causal)
        grad_mixing = (scores * weights).astype(BF16)
        state = state_ref[h * slices : (h + 1) * slices].reshape(HD, HD).astype(BF16)
        across = grown[:, h : h + 1] * dot(grad, state, NT)
        grad_q_ref[:, c] = (dot(grad_mixing, k_ref[:, c], NN) + across).astype(BF16)
        grad_k_ref[:, c] = dot(grad_mixing, q_ref[:, c], TN)
        grad_v_ref[:, c] = dot(mixing_ref[h], grad, TN)


def finish_kernel(
    k_ref, v_ref, state_ref, remain_ref, part_k_ref, part_v_ref, grad_k_ref, grad_v_ref
):
    heads = remain_ref.shape[1]
    slices = state_ref.shape[0] // heads
    remain = remain_ref[...]
    for h in range(heads):
        c = cols(h)
        state = state_ref[h * slices : (h + 1) * slices].reshape(HD, HD).astype(BF16)
        keep = remain[:, h : h + 1]
        grad_k_ref[:, c] = (part_k_ref[:, c] + keep * dot(v_ref[:, c], state, NT)).astype(BF16)
        grad_v_ref[:, c] = (part_v_ref[:, c] + keep * dot(k_ref[:, c], state, NN)).astype(BF16)


def call(kernel, outs, *args, flops=0, limit=16):
    moved = sum(a.size * a.dtype.itemsize for a in args)
    moved += sum(s.size * s.dtype.itemsize for s in outs)
    vmem = pl.BlockSpec(memory_space=pltpu.VMEM)
    return pl.pallas_call(
        kernel,
        out_shape=tuple(outs),
        in_specs=[vmem] * len(args),
        out_specs=tuple([vmem] * len(outs)),
        compiler_params=pltpu.CompilerParams(vmem_limit_bytes=limit * MIB),
        cost_estimate=pl.CostEstimate(flops=flops, bytes_accessed=moved, transcendentals=0),
        name=kernel.__name__,
    )(*args)


def shape(dims, dtype=F32):
    return jax.ShapeDtypeStruct(dims, dtype)


def shards(queries, key_rows, value_rows, log_decay, gate_input, out_gain, prior_state, out_grad):
    tokens, features = queries.shape
    heads = log_decay.shape[1]
    count = lax.axis_size("seq")
    peers = lax.axis_size("head")
    rows = heads * HD // count
    piece = (count, rows, HD)
    wide = (tokens, features)
    gain = out_gain[None, :]
    product = 2 * tokens * HD * HD * heads

    parts, remain = call(
        state_kernel,
        [shape((count, rows + 8, HD)), shape((tokens, heads))],
        key_rows, value_rows, log_decay, flops=product,
    )
    parts = lax.all_to_all(parts, "seq", 0, 0)
    within, mixing, norm_grad, grown = call(
        within_kernel,
        [shape(wide), shape((heads, tokens, tokens), BF16), shape(wide), shape((tokens, heads))],
        queries, key_rows, value_rows, log_decay, gate_input, out_grad, gain,
        flops=4 * product, limit=24,
    )
    prior = lax.dynamic_index_in_dim(prior_state.reshape(piece), lax.axis_index("seq"), 0)
    opening, factor = call(
        forward_chain_kernel, [shape(piece), shape((count, 8, HD))], parts, prior
    )
    opening = lax.all_to_all(opening, "seq", 0, 0)
    context, sums = call(
        context_kernel,
        [shape(wide), shape((peers, 8, tokens))],
        queries, within, norm_grad, grown, opening, flops=product,
    )
    sums = lax.all_to_all(sums, "head", 0, 0)
    grad, parts, inverse = call(
        gradient_kernel,
        [shape(wide, BF16), shape(piece), shape((tokens, HD))],
        sums, queries, context, norm_grad, grown, flops=product,
    )
    parts = lax.all_to_all(parts, "seq", 0, 0)
    attended, grad_gate, grad_query, part_k, part_v = call(
        local_backward_kernel,
        [shape(wide, BF16), shape(wide, BF16), shape(wide, BF16), shape(wide), shape(wide)],
        queries, key_rows, value_rows, grad, opening, mixing, log_decay, grown,
        gate_input, norm_grad, context, gain, inverse,
        flops=9 * product, limit=24,
    )
    (returned,) = call(backward_chain_kernel, [shape(piece)], parts, factor)
    returned = lax.all_to_all(returned, "seq", 0, 0)
    grad_key, grad_value = call(
        finish_kernel,
        [shape(wide, BF16), shape(wide, BF16)],
        key_rows, value_rows, returned, remain, part_k, part_v, flops=2 * product,
    )
    return attended, grad_query, grad_key, grad_value, grad_gate


def solution(mesh):
    wide = P("seq", "head")
    return jax.shard_map(
        shards,
        mesh=mesh,
        in_specs=(wide, wide, wide, wide, wide, P("head"), P("head", None, None), wide),
        out_specs=(wide,) * 5,
        check_vma=False,
    )
```

```python
import jax
import jax.numpy as jnp
from jax import lax
from jax.experimental import pallas as pl
from jax.experimental.pallas import tpu as pltpu
from jax.sharding import PartitionSpec as P

D = 8192
HD = 128
epsilon = 1e-06

F32 = jnp.float32
BF16 = jnp.bfloat16
MIB = 1 << 20


def dot(left, right, dims, precision=None):
    return lax.dot_general(
        left, right, (dims, ((), ())), precision=precision, preferred_element_type=F32
    )


NN = ((1,), (0,))
NT = ((1,), (1,))
TN = ((0,), (0,))


def cols(h):
    return slice(h * HD, (h + 1) * HD)


def token_sums(table, decay):
    return dot(table.astype(F32), decay, NT, lax.Precision.HIGHEST)


def square_iota(n):
    row = lax.broadcasted_iota(jnp.int32, (n, n), 0)
    col = lax.broadcasted_iota(jnp.int32, (n, n), 1)
    return row, col


def state_kernel(io, k_ref, v_ref, decay_ref, out_ref, remain_ref):
    heads, tokens = decay_ref.shape
    row, col = square_iota(tokens)
    decay = decay_ref[...]
    remain = jnp.exp(token_sums(col > row, decay))
    remain_ref[...] = remain
    closing = jnp.sum(decay, axis=1, keepdims=True)
    for h in range(heads):
        io.need(h)
        scaled = (v_ref[:, cols(h)].astype(F32) * remain[:, h : h + 1]).astype(BF16)
        out_ref[h, 0:HD, :] = dot(k_ref[:, cols(h)], scaled, TN)
        out_ref[h, HD : HD + 8, :] = jnp.broadcast_to(closing[h : h + 1], (8, HD))
        io.send(h)


def forward_total_kernel(io, parts_ref, total_ref, factor_ref):
    members = parts_ref.shape[0]
    carried = parts_ref[0, 0:HD, :]
    length = parts_ref[0, HD : HD + 8, :]
    factor_ref[0] = jnp.exp(length)
    for m in range(1, members):
        closing = parts_ref[m, HD : HD + 8, :]
        factor = jnp.exp(closing)
        factor_ref[m] = factor
        length = length + closing
        carried = factor[0:1] * carried + parts_ref[m, 0:HD, :]
    for g in range(total_ref.shape[0]):
        total_ref[g, 0:HD, :] = carried
        total_ref[g, HD : HD + 8, :] = length


def forward_chain_kernel(io, parts_ref, total_ref, factor_ref, prior_ref, out_ref, group_ref):
    members = parts_ref.shape[0]
    groups = total_ref.shape[0]
    here = lax.div(lax.axis_index("seq"), members)
    carried = prior_ref[0]
    for g in range(groups):
        factor = jnp.exp(total_ref[g, HD : HD + 8, :])
        group_ref[g] = factor
        if g < groups - 1:
            later = factor[0:1] * carried + total_ref[g, 0:HD, :]
            carried = jnp.where(g < here, later, carried)
    for m in range(members):
        out_ref[m] = carried
        if m < members - 1:
            carried = factor_ref[m, 0:1, :] * carried + parts_ref[m, 0:HD, :]


def backward_total_kernel(io, parts_ref, factor_ref, total_ref):
    members = parts_ref.shape[0]
    returned = parts_ref[members - 1]
    for m in range(members - 2, -1, -1):
        returned = factor_ref[m, 0:1, :] * returned + parts_ref[m]
    for g in range(total_ref.shape[0]):
        total_ref[g] = returned


def backward_chain_kernel(io, parts_ref, total_ref, factor_ref, group_ref, out_ref):
    members = parts_ref.shape[0]
    groups = total_ref.shape[0]
    here = lax.div(lax.axis_index("seq"), members)
    returned = jnp.zeros((HD, HD), F32)
    for g in range(groups - 1, 0, -1):
        earlier = group_ref[g, 0:1, :] * returned + total_ref[g]
        returned = jnp.where(g > here, earlier, returned)
    for m in range(members - 1, -1, -1):
        out_ref[m] = returned
        if m > 0:
            returned = factor_ref[m, 0:1, :] * returned + parts_ref[m]


def running_tables(decay, causal):
    rows = dot(decay, causal.astype(F32), NT, lax.Precision.HIGHEST)
    return token_sums(causal, decay), rows


def head_weights(running, running_rows, h, causal):
    spread = running[:, h : h + 1] - running_rows[h : h + 1, :]
    return jnp.where(causal, jnp.exp(jnp.minimum(spread, 0.0)), 0.0)


def within_kernel(
    io, q_ref, k_ref, v_ref, gate_ref, grad_ref, decay_ref, gain_ref,
    within_ref, norm_grad_ref, mixing_ref, grown_ref,
):
    heads, tokens = decay_ref.shape
    row, col = square_iota(tokens)
    causal = row >= col
    running, running_rows = running_tables(decay_ref[...], causal)
    grown_ref[...] = jnp.exp(running)
    for h in range(heads):
        io.need(h)
        c = cols(h)
        scores = dot(q_ref[:, c], k_ref[:, c], NT)
        mixing = (scores * head_weights(running, running_rows, h, causal)).astype(BF16)
        mixing_ref[h] = mixing
        within_ref[:, c] = dot(mixing, v_ref[:, c], NN)
        opened = jax.nn.sigmoid(gate_ref[:, c].astype(F32))
        norm_grad_ref[:, c] = grad_ref[:, c].astype(F32) * gain_ref[:, c] * opened
        io.send(h)


def context_kernel(
    io, q_ref, within_ref, norm_grad_ref, grown_ref, state_ref, context_ref, sums_ref
):
    tokens, heads = grown_ref.shape
    grown = grown_ref[...]
    squares = jnp.zeros((tokens, HD), F32)
    products = jnp.zeros((tokens, HD), F32)
    for h in range(heads):
        io.need(h)
        c = cols(h)
        across = dot(q_ref[:, c], state_ref[h].astype(BF16), NN)
        context = within_ref[:, c] + grown[:, h : h + 1] * across
        context_ref[:, c] = context
        squares += context * context
        products += context * norm_grad_ref[:, c]
    ones = jnp.ones((8, HD), F32)
    square_rows = dot(ones, squares, NT, lax.Precision.HIGHEST)
    product_rows = dot(ones, products, NT, lax.Precision.HIGHEST)
    first = lax.broadcasted_iota(jnp.int32, square_rows.shape, 0) == 0
    both = jnp.where(first, square_rows, product_rows)
    for p in range(sums_ref.shape[0]):
        sums_ref[p] = both


def gradient_kernel(
    io, q_ref, norm_grad_ref, sums_ref, context_ref, grown_ref, out_ref, grad_ref, inverse_ref
):
    tokens, heads = grown_ref.shape
    total = sums_ref[0]
    for p in range(1, sums_ref.shape[0]):
        total = total + sums_ref[p]
    pick = lax.broadcasted_iota(jnp.int32, (8, HD), 0)
    square = dot(total, (pick == 0).astype(F32), TN, lax.Precision.HIGHEST)
    product = dot(total, (pick == 1).astype(F32), TN, lax.Precision.HIGHEST)
    inverse = lax.rsqrt(square / D + epsilon)
    inverse_ref[...] = inverse
    slope = inverse * inverse * inverse * product / D
    grown = grown_ref[...]
    for h in range(heads):
        io.need(h)
        c = cols(h)
        grad = (inverse * norm_grad_ref[:, c] - context_ref[:, c] * slope).astype(BF16)
        grad_ref[:, c] = grad
        scaled = (q_ref[:, c].astype(F32) * grown[:, h : h + 1]).astype(BF16)
        out_ref[h] = dot(scaled, grad, TN)
        io.send(h)


def gate_kernel(
    io, gate_ref, norm_grad_ref, context_ref, gain_ref, inverse_ref, attended_ref, grad_gate_ref
):
    heads = context_ref.shape[1] // HD
    inverse = inverse_ref[...]
    for h in range(heads):
        io.need(h)
        c = cols(h)
        opened = jax.nn.sigmoid(gate_ref[:, c].astype(F32))
        normed = context_ref[:, c] * inverse
        attended_ref[:, c] = (normed * gain_ref[:, c] * opened).astype(BF16)
        grad_gate_ref[:, c] = (norm_grad_ref[:, c] * normed * (1.0 - opened)).astype(BF16)
        io.send(h)


def local_backward_kernel(
    io, q_ref, k_ref, v_ref, grad_ref, mixing_ref, state_ref, decay_ref, grown_ref,
    grad_q_ref, grad_k_ref, grad_v_ref,
):
    heads, tokens = decay_ref.shape
    row, col = square_iota(tokens)
    causal = row >= col
    running, running_rows = running_tables(decay_ref[...], causal)
    grown = grown_ref[...]
    for h in range(heads):
        io.need(h)
        c = cols(h)
        grad = grad_ref[:, c]
        scores = dot(grad, v_ref[:, c], NT)
        weights = head_weights(running, running_rows, h, causal)
        grad_mixing = (scores * weights).astype(BF16)
        across = grown[:, h : h + 1] * dot(grad, state_ref[h].astype(BF16), NT)
        grad_q_ref[:, c] = (dot(grad_mixing, k_ref[:, c], NN) + across).astype(BF16)
        grad_k_ref[:, c] = dot(grad_mixing, q_ref[:, c], TN)
        grad_v_ref[:, c] = dot(mixing_ref[h], grad, TN)
        io.send(h)


def finish_kernel(
    io, k_ref, v_ref, part_k_ref, part_v_ref, state_ref, remain_ref, grad_k_ref, grad_v_ref
):
    heads = remain_ref.shape[1]
    remain = remain_ref[...]
    for h in range(heads):
        io.need(h)
        c = cols(h)
        state = state_ref[h].astype(BF16)
        keep = remain[:, h : h + 1]
        grad_k_ref[:, c] = (part_k_ref[:, c] + keep * dot(v_ref[:, c], state, NT)).astype(BF16)
        grad_v_ref[:, c] = (part_v_ref[:, c] + keep * dot(k_ref[:, c], state, NN)).astype(BF16)
        io.send(h)


PAIR = 2


class Stream:
    def __init__(self, chunks, arrivals, departures):
        self.chunks, self.arrivals, self.departures = chunks, arrivals, departures
        for i in range(chunks):
            for copy in arrivals:
                copy(i).start()

    def need(self, h):
        if h % PAIR == 0:
            for copy in self.arrivals:
                copy(h // PAIR).wait()

    def send(self, h):
        if h % PAIR == PAIR - 1:
            for copy in self.departures:
                copy(h // PAIR).start()

    def finish(self):
        for i in range(self.chunks):
            for copy in self.departures:
                copy(i).wait()


def chunk_of(ref, i):
    if len(ref.shape) == 3:
        return ref.at[pl.ds(i * PAIR, PAIR)]
    return ref.at[:, pl.ds(i * PAIR * HD, PAIR * HD)]


def copier(source, target, sem, n):
    return lambda i: pltpu.make_async_copy(chunk_of(source, i), chunk_of(target, i), sem.at[n, i])


def call(kernel, outs, *args, stream_in=0, stream_out=0, chunks=1, flops=0, limit=16):
    moved = sum(a.size * a.dtype.itemsize for a in args)
    moved += sum(s.size * s.dtype.itemsize for s in outs)
    inside = pl.BlockSpec(memory_space=pltpu.VMEM)
    outside = pl.BlockSpec(memory_space=pltpu.HBM)
    n, m = len(args), len(outs)

    def body(*refs):
        ins, results, scratch = list(refs[:n]), list(refs[n : n + m]), refs[n + m :]
        arrivals, departures = [], []
        for j in range(stream_in):
            arrivals.append(copier(ins[j], scratch[j], scratch[-2], j))
            ins[j] = scratch[j]
        for j in range(stream_out):
            local = scratch[stream_in + j]
            departures.append(copier(local, results[j], scratch[-1], j))
            results[j] = local
        io = Stream(chunks, arrivals, departures)
        kernel(io, *ins, *results)
        io.finish()

    streamed = list(args[:stream_in]) + list(outs[:stream_out])
    args = [
        pltpu.with_memory_space_constraint(a, pltpu.HBM) if j < stream_in else a
        for j, a in enumerate(args)
    ]
    shapes = [pltpu.HBM(s.shape, s.dtype) if j < stream_out else s for j, s in enumerate(outs)]
    return pl.pallas_call(
        body,
        out_shape=tuple(shapes),
        in_specs=[outside] * stream_in + [inside] * (n - stream_in),
        out_specs=tuple([outside] * stream_out + [inside] * (m - stream_out)),
        scratch_shapes=[pltpu.VMEM(s.shape, s.dtype) for s in streamed]
        + [
            pltpu.SemaphoreType.DMA((max(stream_in, 1), chunks)),
            pltpu.SemaphoreType.DMA((max(stream_out, 1), chunks)),
        ],
        compiler_params=pltpu.CompilerParams(vmem_limit_bytes=limit * MIB),
        cost_estimate=pl.CostEstimate(flops=flops, bytes_accessed=moved, transcendentals=0),
        name=kernel.__name__,
    )(*args)


def shape(dims, dtype=F32):
    return jax.ShapeDtypeStruct(dims, dtype)


def shards(queries, key_rows, value_rows, log_decay, gate_input, out_gain, prior_state, out_grad):
    tokens, features = queries.shape
    heads = log_decay.shape[1]
    count = lax.axis_size("seq")
    peers = lax.axis_size("head")
    groups = count // heads
    near = [[g * heads + m for m in range(heads)] for g in range(groups)]
    far = [[g * heads + m for g in range(groups)] for m in range(heads)]
    wide = (tokens, features)
    states = (heads, HD, HD)
    gain = out_gain[None, :]
    decay = log_decay.T
    product = 2 * tokens * HD * HD * heads
    chunks = heads // PAIR

    def exchange(value, axis, members=None):
        return lax.all_to_all(value, axis, 0, 0, axis_index_groups=members)

    parts, remain = call(
        state_kernel,
        [shape((heads, HD + 8, HD)), shape((tokens, heads))],
        key_rows, value_rows, decay, stream_in=2, chunks=chunks, flops=product,
    )
    parts = exchange(parts, "seq", near)
    total, factor = call(
        forward_total_kernel, [shape((groups, HD + 8, HD)), shape((heads, 8, HD))], parts
    )
    total = exchange(total, "seq", far)
    within, norm_grad, mixing, grown = call(
        within_kernel,
        [shape(wide), shape(wide), shape((heads, tokens, tokens), BF16), shape((tokens, heads))],
        queries, key_rows, value_rows, gate_input, out_grad, decay, gain,
        stream_in=5, stream_out=3, chunks=chunks, flops=4 * product, limit=24,
    )
    place = lax.rem(lax.axis_index("seq"), heads)
    prior = lax.dynamic_index_in_dim(prior_state, place, 0)
    opening, group_factor = call(
        forward_chain_kernel,
        [shape(states), shape((groups, 8, HD))],
        parts, total, factor, prior,
    )
    opening = exchange(opening, "seq", near)
    context, sums = call(
        context_kernel,
        [shape(wide), shape((peers, 8, tokens))],
        queries, within, norm_grad, grown, opening,
        stream_in=3, chunks=chunks, flops=product,
    )
    sums = exchange(sums, "head")
    parts, grad, inverse = call(
        gradient_kernel,
        [shape(states), shape(wide, BF16), shape((tokens, HD))],
        queries, norm_grad, sums, context, grown,
        stream_in=2, chunks=chunks, flops=product,
    )
    parts = exchange(parts, "seq", near)
    attended, grad_gate = call(
        gate_kernel,
        [shape(wide, BF16), shape(wide, BF16)],
        gate_input, norm_grad, context, gain, inverse,
        stream_in=3, stream_out=2, chunks=chunks, flops=product,
    )
    grad_query, part_k, part_v = call(
        local_backward_kernel,
        [shape(wide, BF16), shape(wide), shape(wide)],
        queries, key_rows, value_rows, grad, mixing, opening, decay, grown,
        stream_in=6, stream_out=3, chunks=chunks, flops=9 * product, limit=24,
    )
    (total,) = call(backward_total_kernel, [shape((groups, HD, HD))], parts, factor)
    total = exchange(total, "seq", far)
    (returned,) = call(
        backward_chain_kernel, [shape(states)], parts, total, factor, group_factor
    )
    returned = exchange(returned, "seq", near)
    grad_key, grad_value = call(
        finish_kernel,
        [shape(wide, BF16), shape(wide, BF16)],
        key_rows, value_rows, part_k, part_v, returned, remain,
        stream_in=4, stream_out=2, chunks=chunks, flops=2 * product,
    )
    return attended, grad_query, grad_key, grad_value, grad_gate


def solution(mesh):
    wide = P("seq", "head")
    return jax.shard_map(
        shards,
        mesh=mesh,
        in_specs=(wide, wide, wide, wide, wide, P("head"), P("head", None, None), wide),
        out_specs=(wide,) * 5,
        check_vma=False,
    )
```

```python
import jax
import jax.numpy as jnp
from jax import lax
from jax.experimental import pallas as pl
from jax.experimental.pallas import tpu as pltpu
from jax.sharding import PartitionSpec as P

D = 8192
HD = 128
epsilon = 1e-06

F32 = jnp.float32
BF16 = jnp.bfloat16
MIB = 1 << 20


def dot(left, right, dims, precision=None):
    return lax.dot_general(
        left, right, (dims, ((), ())), precision=precision, preferred_element_type=F32
    )


NN = ((1,), (0,))
NT = ((1,), (1,))
TN = ((0,), (0,))


def cols(h):
    return slice(h * HD, (h + 1) * HD)


def token_sums(table, decay):
    return dot(table.astype(F32), decay, NT, lax.Precision.HIGHEST)


def square_iota(n):
    row = lax.broadcasted_iota(jnp.int32, (n, n), 0)
    col = lax.broadcasted_iota(jnp.int32, (n, n), 1)
    return row, col


def state_kernel(io, k_ref, v_ref, decay_hbm, out_ref, remain_ref):
    heads, tokens = decay_hbm.shape
    row, col = square_iota(tokens)
    decay = io.fetch(decay_hbm)[...]
    remain = jnp.exp(token_sums(col > row, decay))
    remain_ref[...] = remain
    closing = jnp.sum(decay, axis=1, keepdims=True)
    for h in range(heads):
        io.need(h)
        scaled = (v_ref[:, cols(h)].astype(F32) * remain[:, h : h + 1]).astype(BF16)
        out_ref[h, 0:HD, :] = dot(k_ref[:, cols(h)], scaled, TN)
        out_ref[h, HD : HD + 8, :] = jnp.broadcast_to(closing[h : h + 1], (8, HD))
        io.send(h)


def forward_total_kernel(io, unread, parts_ref, total_ref, factor_ref):
    members = parts_ref.shape[0]
    carried = parts_ref[0, 0:HD, :]
    length = parts_ref[0, HD : HD + 8, :]
    factor_ref[0] = jnp.exp(length)
    for m in range(1, members):
        closing = parts_ref[m, HD : HD + 8, :]
        factor = jnp.exp(closing)
        factor_ref[m] = factor
        length = length + closing
        carried = factor[0:1] * carried + parts_ref[m, 0:HD, :]
    for g in range(total_ref.shape[0]):
        total_ref[g, 0:HD, :] = carried
        total_ref[g, HD : HD + 8, :] = length


def forward_chain_kernel(io, parts_ref, total_ref, factor_ref, prior_ref, out_ref, group_ref):
    members = parts_ref.shape[0]
    groups = total_ref.shape[0]
    here = lax.div(lax.axis_index("seq"), members)
    carried = prior_ref[0]
    for g in range(groups):
        factor = jnp.exp(total_ref[g, HD : HD + 8, :])
        group_ref[g] = factor
        if g < groups - 1:
            later = factor[0:1] * carried + total_ref[g, 0:HD, :]
            carried = jnp.where(g < here, later, carried)
    for m in range(members):
        out_ref[m] = carried
        if m < members - 1:
            carried = factor_ref[m, 0:1, :] * carried + parts_ref[m, 0:HD, :]


def backward_total_kernel(io, unread, also_unread, parts_ref, factor_ref, total_ref):
    members = parts_ref.shape[0]
    returned = parts_ref[members - 1]
    for m in range(members - 2, -1, -1):
        returned = factor_ref[m, 0:1, :] * returned + parts_ref[m]
    for g in range(total_ref.shape[0]):
        total_ref[g] = returned


def backward_chain_kernel(io, parts_ref, total_ref, factor_ref, group_ref, out_ref):
    members = parts_ref.shape[0]
    groups = total_ref.shape[0]
    here = lax.div(lax.axis_index("seq"), members)
    returned = jnp.zeros((HD, HD), F32)
    for g in range(groups - 1, 0, -1):
        earlier = group_ref[g, 0:1, :] * returned + total_ref[g]
        returned = jnp.where(g > here, earlier, returned)
    for m in range(members - 1, -1, -1):
        out_ref[m] = returned
        if m > 0:
            returned = factor_ref[m, 0:1, :] * returned + parts_ref[m]


def running_tables(decay, tokens):
    row, col = square_iota(tokens)
    upto = row >= col
    rows = dot(decay, upto.astype(F32), NT, lax.Precision.HIGHEST)
    return token_sums(upto, decay), rows, row <= col


def head_weights(running, running_rows, h, causal):
    spread = running_rows[h : h + 1, :] - running[:, h : h + 1]
    return jnp.where(causal, jnp.exp(jnp.minimum(spread, 0.0)), 0.0)


def within_kernel(
    io, q_ref, k_ref, v_ref, gate_ref, grad_ref, prior_hbm, decay_ref, gain_ref,
    within_ref, norm_grad_ref, mixing_ref, grown_ref, prior_ref,
):
    heads, tokens = decay_ref.shape
    place = lax.rem(lax.axis_index("seq"), heads)
    prior = io.copy(prior_hbm.at[pl.ds(place, 1)], prior_ref)
    running, running_rows, causal = running_tables(decay_ref[...], tokens)
    grown_ref[...] = jnp.exp(running)
    for h in range(heads):
        io.need(h)
        c = cols(h)
        scores = dot(k_ref[:, c], q_ref[:, c], NT)
        mixing = (scores * head_weights(running, running_rows, h, causal)).astype(BF16)
        mixing_ref[h] = mixing
        within_ref[:, c] = dot(mixing, v_ref[:, c], TN)
        opened = jax.nn.sigmoid(gate_ref[:, c].astype(F32))
        norm_grad_ref[:, c] = grad_ref[:, c].astype(F32) * gain_ref[:, c] * opened
        io.send(h)
    prior.wait()


def context_kernel(
    io, q_ref, within_ref, norm_grad_ref, grown_ref, state_ref, context_ref, sums_ref
):
    tokens, heads = grown_ref.shape
    grown = grown_ref[...]
    squares = jnp.zeros((tokens, HD), F32)
    products = jnp.zeros((tokens, HD), F32)
    for h in range(heads):
        io.need(h)
        c = cols(h)
        across = dot(q_ref[:, c], state_ref[h].astype(BF16), NN)
        context = within_ref[:, c] + grown[:, h : h + 1] * across
        context_ref[:, c] = context
        squares += context * context
        products += context * norm_grad_ref[:, c]
    ones = jnp.ones((8, HD), F32)
    square_rows = dot(ones, squares, NT, lax.Precision.HIGHEST)
    product_rows = dot(ones, products, NT, lax.Precision.HIGHEST)
    first = lax.broadcasted_iota(jnp.int32, square_rows.shape, 0) == 0
    both = jnp.where(first, square_rows, product_rows)
    for p in range(sums_ref.shape[0]):
        sums_ref[p] = both


def gradient_kernel(
    io, q_ref, norm_grad_ref, sums_ref, context_ref, grown_ref, out_ref, grad_ref, inverse_ref,
):
    tokens, heads = grown_ref.shape
    total = sums_ref[0]
    for p in range(1, sums_ref.shape[0]):
        total = total + sums_ref[p]
    pick = lax.broadcasted_iota(jnp.int32, (8, HD), 0)
    square = dot(total, (pick == 0).astype(F32), TN, lax.Precision.HIGHEST)
    product = dot(total, (pick == 1).astype(F32), TN, lax.Precision.HIGHEST)
    inverse = lax.rsqrt(square / D + epsilon)
    inverse_ref[...] = inverse
    slope = inverse * inverse * inverse * product / D
    grown = grown_ref[...]
    for h in range(heads):
        io.need(h)
        c = cols(h)
        grad = (inverse * norm_grad_ref[:, c] - context_ref[:, c] * slope).astype(BF16)
        grad_ref[:, c] = grad
        scaled = (q_ref[:, c].astype(F32) * grown[:, h : h + 1]).astype(BF16)
        out_ref[h] = dot(scaled, grad, TN)
        io.send(h)


def gate_kernel(
    io, gate_ref, norm_grad_ref, context_ref, gain_ref, inverse_ref, attended_ref, grad_gate_ref
):
    heads = context_ref.shape[1] // HD
    inverse = inverse_ref[...]
    for h in range(heads):
        io.need(h)
        c = cols(h)
        opened = jax.nn.sigmoid(gate_ref[:, c].astype(F32))
        normed = context_ref[:, c] * inverse
        attended_ref[:, c] = (normed * gain_ref[:, c] * opened).astype(BF16)
        grad_gate_ref[:, c] = (norm_grad_ref[:, c] * normed * (1.0 - opened)).astype(BF16)
        io.send(h)


def local_backward_kernel(
    io, q_ref, k_ref, v_ref, grad_ref, mixing_ref, state_ref, decay_ref, grown_ref,
    grad_q_ref, grad_k_ref, grad_v_ref,
):
    heads, tokens = decay_ref.shape
    running, running_rows, causal = running_tables(decay_ref[...], tokens)
    grown = grown_ref[...]
    for h in range(heads):
        io.need(h)
        c = cols(h)
        grad = grad_ref[:, c]
        scores = dot(v_ref[:, c], grad, NT)
        weights = head_weights(running, running_rows, h, causal)
        grad_mixing = (scores * weights).astype(BF16)
        across = grown[:, h : h + 1] * dot(grad, state_ref[h].astype(BF16), NT)
        grad_q_ref[:, c] = (dot(grad_mixing, k_ref[:, c], TN) + across).astype(BF16)
        grad_k_ref[:, c] = dot(grad_mixing, q_ref[:, c], NN)
        grad_v_ref[:, c] = dot(mixing_ref[h], grad, NN)
        io.send(h)


def finish_kernel(
    io, k_ref, v_ref, part_k_ref, part_v_ref, state_ref, remain_ref, grad_k_ref, grad_v_ref
):
    heads = remain_ref.shape[1]
    remain = remain_ref[...]
    for h in range(heads):
        io.need(h)
        c = cols(h)
        state = state_ref[h].astype(BF16)
        keep = remain[:, h : h + 1]
        grad_k_ref[:, c] = (part_k_ref[:, c] + keep * dot(v_ref[:, c], state, NT)).astype(BF16)
        grad_v_ref[:, c] = (part_v_ref[:, c] + keep * dot(k_ref[:, c], state, NN)).astype(BF16)
        io.send(h)


PAIR = 2


class Stream:
    def __init__(self, chunks, arrivals, departures, spare, sem):
        self.chunks, self.arrivals, self.departures = chunks, arrivals, departures
        self.spare, self.sem = spare, sem
        if spare is not None:
            self.early = self.copy(*spare)
        for i in range(chunks):
            for copy in arrivals:
                copy(i).start()

    def copy(self, source, target):
        copy = pltpu.make_async_copy(source, target, self.sem)
        copy.start()
        return copy

    def fetch(self, source):
        self.early.wait()
        return self.spare[1]

    def need(self, h):
        if h % PAIR == 0:
            for copy in self.arrivals:
                copy(h // PAIR).wait()

    def send(self, h):
        if h % PAIR == PAIR - 1:
            for copy in self.departures:
                copy(h // PAIR).start()

    def finish(self):
        for i in range(self.chunks):
            for copy in self.departures:
                copy(i).wait()


def chunk_of(ref, i):
    if len(ref.shape) == 3:
        return ref.at[pl.ds(i * PAIR, PAIR)]
    return ref.at[:, pl.ds(i * PAIR * HD, PAIR * HD)]


def copier(source, target, sem, n):
    return lambda i: pltpu.make_async_copy(chunk_of(source, i), chunk_of(target, i), sem.at[n, i])


def call(
    kernel, outs, *args, stream_in=0, raw=0, fetch=False, stream_out=0, chunks=1, flops=0, limit=16
):
    moved = sum(a.size * a.dtype.itemsize for a in args)
    moved += sum(s.size * s.dtype.itemsize for s in outs)
    inside = pl.BlockSpec(memory_space=pltpu.VMEM)
    outside = pl.BlockSpec(memory_space=pltpu.HBM)
    n, m = len(args), len(outs)

    def body(*refs):
        ins, results, scratch = list(refs[:n]), list(refs[n : n + m]), refs[n + m :]
        arrivals, departures = [], []
        for j in range(stream_in):
            arrivals.append(copier(ins[j], scratch[j], scratch[-2], j))
            ins[j] = scratch[j]
        for j in range(stream_out):
            local = scratch[stream_in + j]
            departures.append(copier(local, results[j], scratch[-1], j))
            results[j] = local
        spare = (ins[stream_in], scratch[stream_in + stream_out]) if fetch else None
        io = Stream(chunks, arrivals, departures, spare, scratch[-3].at[0])
        kernel(io, *ins, *results)
        io.finish()

    streamed = list(args[:stream_in]) + list(outs[:stream_out])
    if fetch:
        streamed.append(args[stream_in])
    args = [
        pltpu.with_memory_space_constraint(a, pltpu.HBM) if j < stream_in + raw else a
        for j, a in enumerate(args)
    ]
    shapes = [pltpu.HBM(s.shape, s.dtype) if j < stream_out else s for j, s in enumerate(outs)]
    return pl.pallas_call(
        body,
        out_shape=tuple(shapes),
        in_specs=[outside] * (stream_in + raw) + [inside] * (n - stream_in - raw),
        out_specs=tuple([outside] * stream_out + [inside] * (m - stream_out)),
        scratch_shapes=[pltpu.VMEM(s.shape, s.dtype) for s in streamed]
        + [
            pltpu.SemaphoreType.DMA((1,)),
            pltpu.SemaphoreType.DMA((max(stream_in, 1), chunks)),
            pltpu.SemaphoreType.DMA((max(stream_out, 1), chunks)),
        ],
        compiler_params=pltpu.CompilerParams(vmem_limit_bytes=limit * MIB),
        cost_estimate=pl.CostEstimate(flops=flops, bytes_accessed=moved, transcendentals=0),
        name=kernel.__name__,
    )(*args)


def shape(dims, dtype=F32):
    return jax.ShapeDtypeStruct(dims, dtype)


def shards(queries, key_rows, value_rows, log_decay, gate_input, out_gain, prior_state, out_grad):
    tokens, features = queries.shape
    heads = log_decay.shape[1]
    count = lax.axis_size("seq")
    peers = lax.axis_size("head")
    groups = count // heads
    near = [[g * heads + m for m in range(heads)] for g in range(groups)]
    far = [[g * heads + m for g in range(groups)] for m in range(heads)]
    wide = (tokens, features)
    states = (heads, HD, HD)
    gain = out_gain[None, :]
    decay = log_decay.T
    product = 2 * tokens * HD * HD * heads
    chunks = heads // PAIR

    def exchange(value, axis, members=None):
        return lax.all_to_all(value, axis, 0, 0, axis_index_groups=members)

    parts, remain = call(
        state_kernel,
        [shape((heads, HD + 8, HD)), shape((tokens, heads))],
        key_rows, value_rows, decay,
        stream_in=2, raw=1, fetch=True, stream_out=1, chunks=chunks, flops=product,
    )
    parts = exchange(parts, "seq", near)
    within, norm_grad, mixing, grown, prior = call(
        within_kernel,
        [
            shape(wide), shape(wide), shape((heads, tokens, tokens), BF16),
            shape((tokens, heads)), shape((1, HD, HD)),
        ],
        queries, key_rows, value_rows, gate_input, out_grad, prior_state, decay, gain,
        stream_in=5, raw=1, stream_out=3, chunks=chunks, flops=4 * product, limit=24,
    )
    total, factor = call(
        forward_total_kernel,
        [shape((groups, HD + 8, HD)), shape((heads, 8, HD))],
        within, parts, raw=1,
    )
    total = exchange(total, "seq", far)
    opening, group_factor = call(
        forward_chain_kernel,
        [shape(states), shape((groups, 8, HD))],
        parts, total, factor, prior,
    )
    opening = exchange(opening, "seq", near)
    context, sums = call(
        context_kernel,
        [shape(wide), shape((peers, 8, tokens))],
        queries, within, norm_grad, grown, opening, flops=product,
    )
    sums = exchange(sums, "head")
    parts, grad, inverse = call(
        gradient_kernel,
        [shape(states), shape(wide, BF16), shape((tokens, HD))],
        queries, norm_grad, sums, context, grown,
        stream_out=2, chunks=chunks, flops=product,
    )
    parts = exchange(parts, "seq", near)
    attended, grad_gate = call(
        gate_kernel,
        [shape(wide, BF16), shape(wide, BF16)],
        gate_input, norm_grad, context, gain, inverse,
        stream_in=3, stream_out=2, chunks=chunks, flops=product,
    )
    grad_query, part_k, part_v = call(
        local_backward_kernel,
        [shape(wide, BF16), shape(wide), shape(wide)],
        queries, key_rows, value_rows, grad, mixing, opening, decay, grown,
        stream_in=6, stream_out=3, chunks=chunks, flops=9 * product, limit=24,
    )
    (total,) = call(
        backward_total_kernel,
        [shape((groups, HD, HD))],
        attended, part_k, parts, factor, raw=2,
    )
    total = exchange(total, "seq", far)
    (returned,) = call(
        backward_chain_kernel, [shape(states)], parts, total, factor, group_factor
    )
    returned = exchange(returned, "seq", near)
    grad_key, grad_value = call(
        finish_kernel,
        [shape(wide, BF16), shape(wide, BF16)],
        key_rows, value_rows, part_k, part_v, returned, remain,
        stream_out=2, chunks=chunks, flops=2 * product,
    )
    return attended, grad_query, grad_key, grad_value, grad_gate


def solution(mesh):
    wide = P("seq", "head")
    return jax.shard_map(
        shards,
        mesh=mesh,
        in_specs=(wide, wide, wide, wide, wide, P("head"), P("head", None, None), wide),
        out_specs=(wide,) * 5,
        check_vma=False,
    )
```

```python
import jax
import jax.numpy as jnp
from jax import lax
from jax.experimental import pallas as pl
from jax.experimental.pallas import tpu as pltpu
from jax.sharding import PartitionSpec as P

D = 8192
HD = 128
epsilon = 1e-06

F32 = jnp.float32
BF16 = jnp.bfloat16
MIB = 1 << 20


def dot(left, right, dims, precision=None):
    return lax.dot_general(
        left, right, (dims, ((), ())), precision=precision, preferred_element_type=F32
    )


NN = ((1,), (0,))
NT = ((1,), (1,))
TN = ((0,), (0,))


def cols(h):
    return slice(h * HD, (h + 1) * HD)


def token_sums(table, decay):
    heads = decay.shape[0]
    sums = dot(table.astype(F32).astype(BF16), thirds(decay), NT)
    return sums[:, 0:heads] + sums[:, heads : 2 * heads] + sums[:, 2 * heads : 3 * heads]


def thirds(decay):
    upper = decay.astype(BF16).astype(F32)
    rest = decay - upper
    middle = rest.astype(BF16).astype(F32)
    lower = rest - middle
    return jnp.concatenate([upper, middle, lower], axis=0).astype(BF16)


def square_iota(n):
    row = lax.broadcasted_iota(jnp.int32, (n, n), 0)
    col = lax.broadcasted_iota(jnp.int32, (n, n), 1)
    return row, col


def state_kernel(io, k_ref, v_ref, decay_hbm, out_ref, remain_ref):
    heads, tokens = decay_hbm.shape
    row, col = square_iota(tokens)
    decay = io.fetch(decay_hbm)[...]
    remain = jnp.exp(token_sums(col > row, decay))
    remain_ref[...] = remain
    closing = jnp.sum(decay, axis=1, keepdims=True)
    for h in range(heads):
        io.need(h)
        scaled = (v_ref[:, cols(h)].astype(F32) * remain[:, h : h + 1]).astype(BF16)
        out_ref[h, 0:HD, :] = dot(k_ref[:, cols(h)], scaled, TN)
        out_ref[h, HD : HD + 8, :] = jnp.broadcast_to(closing[h : h + 1], (8, HD))
        io.send(h)


def forward_total_kernel(io, unread, parts_ref, total_ref, factor_ref):
    members = parts_ref.shape[0]
    carried = parts_ref[0, 0:HD, :]
    length = parts_ref[0, HD : HD + 8, :]
    factor_ref[0] = jnp.exp(length)
    for m in range(1, members):
        closing = parts_ref[m, HD : HD + 8, :]
        factor = jnp.exp(closing)
        factor_ref[m] = factor
        length = length + closing
        carried = factor[0:1] * carried + parts_ref[m, 0:HD, :]
    for g in range(total_ref.shape[0]):
        total_ref[g, 0:HD, :] = carried
        total_ref[g, HD : HD + 8, :] = length


def forward_chain_kernel(io, parts_ref, total_ref, factor_ref, prior_ref, out_ref, group_ref):
    members = parts_ref.shape[0]
    groups = total_ref.shape[0]
    here = lax.div(lax.axis_index("seq"), members)
    carried = prior_ref[0]
    for g in range(groups):
        factor = jnp.exp(total_ref[g, HD : HD + 8, :])
        group_ref[g] = factor
        if g < groups - 1:
            later = factor[0:1] * carried + total_ref[g, 0:HD, :]
            carried = jnp.where(g < here, later, carried)
    for m in range(members):
        out_ref[m] = carried
        if m < members - 1:
            carried = factor_ref[m, 0:1, :] * carried + parts_ref[m, 0:HD, :]


def backward_total_kernel(io, unread, parts_ref, factor_ref, total_ref):
    members = parts_ref.shape[0]
    returned = parts_ref[members - 1]
    for m in range(members - 2, -1, -1):
        returned = factor_ref[m, 0:1, :] * returned + parts_ref[m]
    for g in range(total_ref.shape[0]):
        total_ref[g] = returned


def backward_chain_kernel(io, parts_ref, total_ref, factor_ref, group_ref, out_ref):
    members = parts_ref.shape[0]
    groups = total_ref.shape[0]
    here = lax.div(lax.axis_index("seq"), members)
    returned = jnp.zeros((HD, HD), F32)
    for g in range(groups - 1, 0, -1):
        earlier = group_ref[g, 0:1, :] * returned + total_ref[g]
        returned = jnp.where(g > here, earlier, returned)
    for m in range(members - 1, -1, -1):
        out_ref[m] = returned
        if m > 0:
            returned = factor_ref[m, 0:1, :] * returned + parts_ref[m]


def running_tables(decay, tokens):
    row, col = square_iota(tokens)
    upto = row >= col
    heads = decay.shape[0]
    sums = dot(thirds(decay), upto.astype(F32).astype(BF16), NT)
    rows = sums[0:heads] + sums[heads : 2 * heads] + sums[2 * heads : 3 * heads]
    return token_sums(upto, decay), rows, row <= col


def head_weights(running, running_rows, h, causal):
    spread = running_rows[h : h + 1, :] - running[:, h : h + 1]
    return jnp.where(causal, jnp.exp(jnp.minimum(spread, 0.0)), 0.0)


def within_kernel(
    io, q_ref, k_ref, v_ref, gate_ref, grad_ref, prior_hbm, decay_ref, gain_ref,
    within_ref, norm_grad_ref, mixing_ref, query_ref, grown_ref, prior_ref,
):
    heads, tokens = decay_ref.shape
    place = lax.rem(lax.axis_index("seq"), heads)
    prior = io.copy(prior_hbm.at[pl.ds(place, 1)], prior_ref)
    running, running_rows, causal = running_tables(decay_ref[...], tokens)
    grown = jnp.exp(running)
    grown_ref[...] = grown
    for h in range(heads):
        io.need(h)
        c = cols(h)
        scores = dot(k_ref[:, c], q_ref[:, c], NT)
        mixing = (scores * head_weights(running, running_rows, h, causal)).astype(BF16)
        mixing_ref[h] = mixing
        within_ref[:, c] = dot(mixing, v_ref[:, c], TN)
        scaled = (q_ref[:, c].astype(F32) * grown[:, h : h + 1]).astype(BF16)
        query_ref[h] = scaled.T
        opened = jax.nn.sigmoid(gate_ref[:, c].astype(F32))
        norm_grad_ref[:, c] = grad_ref[:, c].astype(F32) * gain_ref[:, c] * opened
        io.send(h)
    prior.wait()


def context_kernel(
    io, q_ref, within_ref, norm_grad_ref, grown_ref, state_ref, context_ref, sums_ref
):
    tokens, heads = grown_ref.shape
    grown = grown_ref[...]
    squares = jnp.zeros((tokens, HD), F32)
    products = jnp.zeros((tokens, HD), F32)
    for h in range(heads):
        io.need(h)
        c = cols(h)
        across = dot(q_ref[:, c], state_ref[h].astype(BF16), NN)
        context = within_ref[:, c] + grown[:, h : h + 1] * across
        context_ref[:, c] = context
        squares += context * context
        products += context * norm_grad_ref[:, c]
    ones = jnp.ones((8, HD), F32)
    square_rows = dot(ones, squares, NT, lax.Precision.HIGHEST)[0:2]
    product_rows = dot(ones, products, NT, lax.Precision.HIGHEST)[0:2]
    first = lax.broadcasted_iota(jnp.int32, square_rows.shape, 0) == 0
    both = jnp.where(first, square_rows, product_rows)
    for p in range(sums_ref.shape[0]):
        sums_ref[p] = both


def gradient_kernel(
    io, query_ref, norm_grad_ref, sums_ref, context_ref, out_ref, inverse_ref, slope_ref
):
    heads = query_ref.shape[0]
    total = sums_ref[0]
    for p in range(1, sums_ref.shape[0]):
        total = total + sums_ref[p]
    pick = lax.broadcasted_iota(jnp.int32, (2, HD), 0)
    square = dot(total, (pick == 0).astype(F32), TN, lax.Precision.HIGHEST)
    product = dot(total, (pick == 1).astype(F32), TN, lax.Precision.HIGHEST)
    inverse = lax.rsqrt(square / D + epsilon)
    slope = inverse * inverse * inverse * product / D
    inverse_ref[...] = inverse
    slope_ref[...] = slope
    for h in range(heads):
        c = cols(h)
        grad = (inverse * norm_grad_ref[:, c] - context_ref[:, c] * slope).astype(BF16)
        out_ref[h] = dot(query_ref[h], grad, NN)
        io.send(h)


def local_backward_kernel(
    io, q_ref, k_ref, v_ref, gate_ref, norm_grad_ref, context_ref, mixing_ref, state_ref,
    decay_ref, grown_ref, gain_ref, inverse_ref, slope_ref,
    attended_ref, grad_gate_ref, grad_q_ref, grad_k_ref, grad_v_ref,
):
    heads, tokens = decay_ref.shape
    running, running_rows, causal = running_tables(decay_ref[...], tokens)
    grown = grown_ref[...]
    inverse = inverse_ref[...]
    slope = slope_ref[...]
    for h in range(heads):
        io.need(h)
        c = cols(h)
        context = context_ref[:, c]
        norm_grad = norm_grad_ref[:, c]
        opened = jax.nn.sigmoid(gate_ref[:, c].astype(F32))
        normed = context * inverse
        attended_ref[:, c] = (normed * gain_ref[:, c] * opened).astype(BF16)
        grad_gate_ref[:, c] = (norm_grad * normed * (1.0 - opened)).astype(BF16)
        grad = (inverse * norm_grad - context * slope).astype(BF16)
        scores = dot(v_ref[:, c], grad, NT)
        weights = head_weights(running, running_rows, h, causal)
        grad_mixing = (scores * weights).astype(BF16)
        across = grown[:, h : h + 1] * dot(grad, state_ref[h].astype(BF16), NT)
        grad_q_ref[:, c] = (dot(grad_mixing, k_ref[:, c], TN) + across).astype(BF16)
        grad_k_ref[:, c] = dot(grad_mixing, q_ref[:, c], NN)
        grad_v_ref[:, c] = dot(mixing_ref[h], grad, NN)
        io.send(h)


def finish_kernel(
    io, k_ref, v_ref, part_k_ref, part_v_ref, state_ref, remain_ref, grad_k_ref, grad_v_ref
):
    heads = remain_ref.shape[1]
    remain = remain_ref[...]
    for h in range(heads):
        io.need(h)
        c = cols(h)
        state = state_ref[h].astype(BF16)
        keep = remain[:, h : h + 1]
        grad_k_ref[:, c] = (part_k_ref[:, c] + keep * dot(v_ref[:, c], state, NT)).astype(BF16)
        grad_v_ref[:, c] = (part_v_ref[:, c] + keep * dot(k_ref[:, c], state, NN)).astype(BF16)
        io.send(h)


PAIR = 2


class Stream:
    def __init__(self, chunks, arrivals, departures, spare, sem):
        self.chunks, self.arrivals, self.departures = chunks, arrivals, departures
        self.spare, self.sem = spare, sem
        if spare is not None:
            self.early = self.copy(*spare)
        for i in range(chunks):
            for copy in arrivals:
                copy(i).start()

    def copy(self, source, target):
        copy = pltpu.make_async_copy(source, target, self.sem)
        copy.start()
        return copy

    def fetch(self, source):
        self.early.wait()
        return self.spare[1]

    def need(self, h):
        if h % PAIR == 0:
            for copy in self.arrivals:
                copy(h // PAIR).wait()

    def send(self, h):
        if h % PAIR == PAIR - 1:
            for copy in self.departures:
                copy(h // PAIR).start()

    def finish(self):
        for i in range(self.chunks):
            for copy in self.departures:
                copy(i).wait()


def chunk_of(ref, i):
    if len(ref.shape) == 3:
        return ref.at[pl.ds(i * PAIR, PAIR)]
    return ref.at[:, pl.ds(i * PAIR * HD, PAIR * HD)]


def copier(source, target, sem, n):
    return lambda i: pltpu.make_async_copy(chunk_of(source, i), chunk_of(target, i), sem.at[n, i])


def call(
    kernel, outs, *args, stream_in=0, raw=0, fetch=False, stream_out=0, chunks=1, flops=0, limit=16
):
    moved = sum(a.size * a.dtype.itemsize for a in args)
    moved += sum(s.size * s.dtype.itemsize for s in outs)
    inside = pl.BlockSpec(memory_space=pltpu.VMEM)
    outside = pl.BlockSpec(memory_space=pltpu.HBM)
    n, m = len(args), len(outs)

    def body(*refs):
        ins, results, scratch = list(refs[:n]), list(refs[n : n + m]), refs[n + m :]
        arrivals, departures = [], []
        for j in range(stream_in):
            arrivals.append(copier(ins[j], scratch[j], scratch[-2], j))
            ins[j] = scratch[j]
        for j in range(stream_out):
            local = scratch[stream_in + j]
            departures.append(copier(local, results[j], scratch[-1], j))
            results[j] = local
        spare = (ins[stream_in], scratch[stream_in + stream_out]) if fetch else None
        io = Stream(chunks, arrivals, departures, spare, scratch[-3].at[0])
        kernel(io, *ins, *results)
        io.finish()

    streamed = list(args[:stream_in]) + list(outs[:stream_out])
    if fetch:
        streamed.append(args[stream_in])
    args = [
        pltpu.with_memory_space_constraint(a, pltpu.HBM) if j < stream_in + raw else a
        for j, a in enumerate(args)
    ]
    shapes = [pltpu.HBM(s.shape, s.dtype) if j < stream_out else s for j, s in enumerate(outs)]
    return pl.pallas_call(
        body,
        out_shape=tuple(shapes),
        in_specs=[outside] * (stream_in + raw) + [inside] * (n - stream_in - raw),
        out_specs=tuple([outside] * stream_out + [inside] * (m - stream_out)),
        scratch_shapes=[pltpu.VMEM(s.shape, s.dtype) for s in streamed]
        + [
            pltpu.SemaphoreType.DMA((1,)),
            pltpu.SemaphoreType.DMA((max(stream_in, 1), chunks)),
            pltpu.SemaphoreType.DMA((max(stream_out, 1), chunks)),
        ],
        compiler_params=pltpu.CompilerParams(vmem_limit_bytes=limit * MIB),
        cost_estimate=pl.CostEstimate(flops=flops, bytes_accessed=moved, transcendentals=0),
        name=kernel.__name__,
    )(*args)


def shape(dims, dtype=F32):
    return jax.ShapeDtypeStruct(dims, dtype)


def shards(queries, key_rows, value_rows, log_decay, gate_input, out_gain, prior_state, out_grad):
    tokens, features = queries.shape
    heads = log_decay.shape[1]
    count = lax.axis_size("seq")
    peers = lax.axis_size("head")
    groups = count // heads
    near = [[g * heads + m for m in range(heads)] for g in range(groups)]
    far = [[g * heads + m for g in range(groups)] for m in range(heads)]
    wide = (tokens, features)
    states = (heads, HD, HD)
    gain = out_gain[None, :]
    decay = log_decay.T
    product = 2 * tokens * HD * HD * heads
    chunks = heads // PAIR

    def exchange(value, axis, members=None):
        return lax.all_to_all(value, axis, 0, 0, axis_index_groups=members)

    parts, remain = call(
        state_kernel,
        [shape((heads, HD + 8, HD)), shape((tokens, heads))],
        key_rows, value_rows, decay,
        stream_in=2, raw=1, fetch=True, stream_out=1, chunks=chunks, flops=product,
    )
    parts = exchange(parts, "seq", near)
    within, norm_grad, mixing, scaled, grown, prior = call(
        within_kernel,
        [
            shape(wide), shape(wide), shape((heads, tokens, tokens), BF16),
            shape((heads, HD, tokens), BF16), shape((tokens, heads)), shape((1, HD, HD)),
        ],
        queries, key_rows, value_rows, gate_input, out_grad, prior_state, decay, gain,
        stream_in=5, raw=1, stream_out=4, chunks=chunks, flops=4 * product, limit=24,
    )
    total, factor = call(
        forward_total_kernel,
        [shape((groups, HD + 8, HD)), shape((heads, 8, HD))],
        within, parts, raw=1,
    )
    total = exchange(total, "seq", far)
    opening, group_factor = call(
        forward_chain_kernel,
        [shape(states), shape((groups, 8, HD))],
        parts, total, factor, prior,
    )
    opening = exchange(opening, "seq", near)
    context, sums = call(
        context_kernel,
        [shape(wide), shape((peers, 2, tokens))],
        queries, within, norm_grad, grown, opening, flops=product,
    )
    sums = exchange(sums, "head")
    parts, inverse, slope = call(
        gradient_kernel,
        [shape(states), shape((tokens, HD)), shape((tokens, HD))],
        scaled, norm_grad, sums, context,
        stream_out=1, chunks=chunks, flops=product,
    )
    parts = exchange(parts, "seq", near)
    attended, grad_gate, grad_query, part_k, part_v = call(
        local_backward_kernel,
        [shape(wide, BF16), shape(wide, BF16), shape(wide, BF16), shape(wide), shape(wide)],
        queries, key_rows, value_rows, gate_input, norm_grad, context, mixing, opening,
        decay, grown, gain, inverse, slope,
        stream_in=8, stream_out=5, chunks=chunks, flops=9 * product, limit=32,
    )
    (total,) = call(
        backward_total_kernel,
        [shape((groups, HD, HD))],
        part_k, parts, factor, raw=1,
    )
    total = exchange(total, "seq", far)
    (returned,) = call(
        backward_chain_kernel, [shape(states)], parts, total, factor, group_factor
    )
    returned = exchange(returned, "seq", near)
    grad_key, grad_value = call(
        finish_kernel,
        [shape(wide, BF16), shape(wide, BF16)],
        key_rows, value_rows, part_k, part_v, returned, remain,
        stream_out=2, chunks=chunks, flops=2 * product,
    )
    return attended, grad_query, grad_key, grad_value, grad_gate


def solution(mesh):
    wide = P("seq", "head")
    return jax.shard_map(
        shards,
        mesh=mesh,
        in_specs=(wide, wide, wide, wide, wide, P("head"), P("head", None, None), wide),
        out_specs=(wide,) * 5,
        check_vma=False,
    )
```

```python
import jax
import jax.numpy as jnp
from jax import lax
from jax.experimental import pallas as pl
from jax.experimental.pallas import tpu as pltpu
from jax.sharding import PartitionSpec as P

D = 8192
HD = 128
epsilon = 1e-06

F32 = jnp.float32
BF16 = jnp.bfloat16
MIB = 1 << 20


def dot(left, right, dims, precision=None):
    return lax.dot_general(
        left, right, (dims, ((), ())), precision=precision, preferred_element_type=F32
    )


NN = ((1,), (0,))
NT = ((1,), (1,))
TN = ((0,), (0,))


def cols(h):
    return slice(h * HD, (h + 1) * HD)


def token_sums(table, decay):
    heads = decay.shape[0]
    sums = dot(table.astype(F32).astype(BF16), thirds(decay), NT)
    return sums[:, 0:heads] + sums[:, heads : 2 * heads] + sums[:, 2 * heads : 3 * heads]


def thirds(decay):
    upper = decay.astype(BF16).astype(F32)
    rest = decay - upper
    middle = rest.astype(BF16).astype(F32)
    lower = rest - middle
    return jnp.concatenate([upper, middle, lower], axis=0).astype(BF16)


def square_iota(n):
    row = lax.broadcasted_iota(jnp.int32, (n, n), 0)
    col = lax.broadcasted_iota(jnp.int32, (n, n), 1)
    return row, col


def state_kernel(io, k_ref, v_ref, decay_hbm, out_ref, remain_ref):
    heads, tokens = decay_hbm.shape
    row, col = square_iota(tokens)
    decay = io.fetch(decay_hbm)[...]
    remain = jnp.exp(token_sums(col > row, decay))
    remain_ref[...] = remain
    closing = jnp.sum(decay, axis=1, keepdims=True)
    for h in range(heads):
        io.need(h)
        scaled = (v_ref[:, cols(h)].astype(F32) * remain[:, h : h + 1]).astype(BF16)
        out_ref[h, 0:HD, :] = dot(k_ref[:, cols(h)], scaled, TN)
        out_ref[h, HD : HD + 8, :] = jnp.broadcast_to(closing[h : h + 1], (8, HD))
        io.send(h)


def forward_total_kernel(io, unread, parts_ref, total_ref, factor_ref):
    members = parts_ref.shape[0]
    carried = parts_ref[0, 0:HD, :]
    length = parts_ref[0, HD : HD + 8, :]
    factor_ref[0] = jnp.exp(length)
    for m in range(1, members):
        closing = parts_ref[m, HD : HD + 8, :]
        factor = jnp.exp(closing)
        factor_ref[m] = factor
        length = length + closing
        carried = factor[0:1] * carried + parts_ref[m, 0:HD, :]
    for g in range(total_ref.shape[0]):
        total_ref[g, 0:HD, :] = carried
        total_ref[g, HD : HD + 8, :] = length


def forward_chain_kernel(io, parts_ref, total_ref, factor_ref, prior_ref, out_ref, group_ref):
    members = parts_ref.shape[0]
    groups = total_ref.shape[0]
    here = lax.div(lax.axis_index("seq"), members)
    carried = prior_ref[0]
    for g in range(groups):
        factor = jnp.exp(total_ref[g, HD : HD + 8, :])
        group_ref[g] = factor
        if g < groups - 1:
            later = factor[0:1] * carried + total_ref[g, 0:HD, :]
            carried = jnp.where(g < here, later, carried)
    for m in range(members):
        out_ref[m] = carried
        if m < members - 1:
            carried = factor_ref[m, 0:1, :] * carried + parts_ref[m, 0:HD, :]


def backward_total_kernel(io, unread, parts_ref, factor_ref, total_ref):
    members = parts_ref.shape[0]
    returned = parts_ref[members - 1]
    for m in range(members - 2, -1, -1):
        returned = factor_ref[m, 0:1, :] * returned + parts_ref[m]
    for g in range(total_ref.shape[0]):
        total_ref[g] = returned


def backward_chain_kernel(io, parts_ref, total_ref, factor_ref, group_ref, out_ref):
    members = parts_ref.shape[0]
    groups = total_ref.shape[0]
    here = lax.div(lax.axis_index("seq"), members)
    returned = jnp.zeros((HD, HD), F32)
    for g in range(groups - 1, 0, -1):
        earlier = group_ref[g, 0:1, :] * returned + total_ref[g]
        returned = jnp.where(g > here, earlier, returned)
    for m in range(members - 1, -1, -1):
        out_ref[m] = returned
        if m > 0:
            returned = factor_ref[m, 0:1, :] * returned + parts_ref[m]


def running_tables(decay, tokens):
    row, col = square_iota(tokens)
    upto = row >= col
    heads = decay.shape[0]
    sums = dot(thirds(decay), upto.astype(F32).astype(BF16), NT)
    rows = sums[0:heads] + sums[heads : 2 * heads] + sums[2 * heads : 3 * heads]
    return token_sums(upto, decay), rows, row <= col


def head_weights(running, running_rows, h, causal):
    spread = running_rows[h : h + 1, :] - running[:, h : h + 1]
    return jnp.where(causal, jnp.exp(jnp.minimum(spread, 0.0)), 0.0)


def within_kernel(
    io, q_ref, k_ref, v_ref, gate_ref, grad_ref, prior_hbm, decay_ref, gain_ref,
    within_ref, norm_grad_ref, mixing_ref, query_ref, grown_ref, prior_ref,
):
    heads, tokens = decay_ref.shape
    place = lax.rem(lax.axis_index("seq"), heads)
    prior = io.copy(prior_hbm.at[pl.ds(place, 1)], prior_ref)
    running, running_rows, causal = running_tables(decay_ref[...], tokens)
    grown = jnp.exp(running)
    grown_ref[...] = grown
    for h in range(heads):
        io.need(h)
        c = cols(h)
        scores = dot(k_ref[:, c], q_ref[:, c], NT)
        mixing = (scores * head_weights(running, running_rows, h, causal)).astype(BF16)
        mixing_ref[h] = mixing
        within_ref[:, c] = dot(mixing, v_ref[:, c], TN)
        scaled = (q_ref[:, c].astype(F32) * grown[:, h : h + 1]).astype(BF16)
        query_ref[h] = scaled.T
        opened = jax.nn.sigmoid(gate_ref[:, c].astype(F32))
        norm_grad_ref[:, c] = grad_ref[:, c].astype(F32) * gain_ref[:, c] * opened
        io.send(h)
    prior.wait()


def context_kernel(
    io, q_ref, within_ref, norm_grad_ref, grown_ref, state_ref, context_ref, sums_ref
):
    tokens, heads = grown_ref.shape
    grown = grown_ref[...]
    squares = jnp.zeros((tokens, HD), F32)
    products = jnp.zeros((tokens, HD), F32)
    for h in range(heads):
        io.need(h)
        c = cols(h)
        across = dot(q_ref[:, c], state_ref[h].astype(BF16), NN)
        context = within_ref[:, c] + grown[:, h : h + 1] * across
        context_ref[:, c] = context
        squares += context * context
        products += context * norm_grad_ref[:, c]
    ones = jnp.ones((8, HD), F32)
    square_rows = dot(ones, squares, NT, lax.Precision.HIGHEST)[0:2]
    product_rows = dot(ones, products, NT, lax.Precision.HIGHEST)[0:2]
    first = lax.broadcasted_iota(jnp.int32, square_rows.shape, 0) == 0
    both = jnp.where(first, square_rows, product_rows)
    for p in range(sums_ref.shape[0]):
        sums_ref[p] = both


def gradient_kernel(
    io, query_ref, norm_grad_ref, sums_ref, context_ref, out_ref, inverse_ref, slope_ref
):
    heads = query_ref.shape[0]
    total = sums_ref[0]
    for p in range(1, sums_ref.shape[0]):
        total = total + sums_ref[p]
    pick = lax.broadcasted_iota(jnp.int32, (2, HD), 0)
    square = dot(total, (pick == 0).astype(F32), TN, lax.Precision.HIGHEST)
    product = dot(total, (pick == 1).astype(F32), TN, lax.Precision.HIGHEST)
    inverse = lax.rsqrt(square / D + epsilon)
    slope = inverse * inverse * inverse * product / D
    inverse_ref[...] = inverse
    slope_ref[...] = slope
    for h in range(heads):
        c = cols(h)
        grad = (inverse * norm_grad_ref[:, c] - context_ref[:, c] * slope).astype(BF16)
        out_ref[h] = dot(query_ref[h], grad, NN)
        io.send(h)


def local_backward_kernel(
    io, q_ref, k_ref, v_ref, gate_ref, norm_grad_ref, context_ref, mixing_ref, state_ref,
    decay_ref, grown_ref, gain_ref, inverse_ref, slope_ref,
    attended_ref, grad_gate_ref, grad_q_ref, grad_k_ref, grad_v_ref,
):
    heads, tokens = decay_ref.shape
    running, running_rows, causal = running_tables(decay_ref[...], tokens)
    grown = grown_ref[...]
    inverse = inverse_ref[...]
    slope = slope_ref[...]
    for h in range(heads):
        io.need(h)
        c = cols(h)
        context = context_ref[:, c]
        norm_grad = norm_grad_ref[:, c]
        opened = jax.nn.sigmoid(gate_ref[:, c].astype(F32))
        normed = context * inverse
        attended_ref[:, c] = (normed * gain_ref[:, c] * opened).astype(BF16)
        grad_gate_ref[:, c] = (norm_grad * normed * (1.0 - opened)).astype(BF16)
        grad = (inverse * norm_grad - context * slope).astype(BF16)
        scores = dot(v_ref[:, c], grad, NT)
        weights = head_weights(running, running_rows, h, causal)
        grad_mixing = (scores * weights).astype(BF16)
        across = grown[:, h : h + 1] * dot(grad, state_ref[h].astype(BF16), NT)
        grad_q_ref[:, c] = (dot(grad_mixing, k_ref[:, c], TN) + across).astype(BF16)
        grad_k_ref[:, c] = dot(grad_mixing, q_ref[:, c], NN)
        grad_v_ref[:, c] = dot(mixing_ref[h], grad, NN)
        io.send(h)


def finish_kernel(
    io, k_ref, v_ref, part_k_ref, part_v_ref, state_ref, remain_ref, grad_k_ref, grad_v_ref
):
    heads = remain_ref.shape[1]
    remain = remain_ref[...]
    for h in range(heads):
        io.need(h)
        c = cols(h)
        state = state_ref[h].astype(BF16)
        keep = remain[:, h : h + 1]
        grad_k_ref[:, c] = (part_k_ref[:, c] + keep * dot(v_ref[:, c], state, NT)).astype(BF16)
        grad_v_ref[:, c] = (part_v_ref[:, c] + keep * dot(k_ref[:, c], state, NN)).astype(BF16)
        io.send(h)


class Stream:
    def __init__(self, heads, bring, take, ahead, arrivals, departures, spare, sem):
        self.heads, self.bring, self.take, self.ahead = heads, bring, take, ahead
        self.arrivals, self.departures = arrivals, departures
        self.spare, self.sem = spare, sem
        if spare is not None:
            self.early = self.copy(*spare)
        for i in range(min(ahead, heads // bring)):
            self.begin(i)

    def begin(self, i):
        for copy in self.arrivals:
            copy(i, self.bring).start()

    def copy(self, source, target):
        copy = pltpu.make_async_copy(source, target, self.sem)
        copy.start()
        return copy

    def fetch(self, source):
        self.early.wait()
        return self.spare[1]

    def need(self, h):
        i, inside = divmod(h, self.bring)
        if inside == 0:
            for copy in self.arrivals:
                copy(i, self.bring).wait()
            if (i + self.ahead) * self.bring < self.heads:
                self.begin(i + self.ahead)

    def send(self, h):
        i, inside = divmod(h, self.take)
        if inside == self.take - 1:
            for copy in self.departures:
                copy(i, self.take).start()

    def finish(self):
        for i in range(self.heads // self.take):
            for copy in self.departures:
                copy(i, self.take).wait()


def run_of(ref, i, n):
    if len(ref.shape) == 3:
        return ref.at[pl.ds(i * n, n)]
    return ref.at[:, pl.ds(i * n * HD, n * HD)]


def copier(source, target, sem, j):
    return lambda i, n: pltpu.make_async_copy(
        run_of(source, i, n), run_of(target, i, n), sem.at[j, i]
    )


def call(
    kernel, outs, *args, stream_in=0, raw=0, fetch=False, stream_out=0,
    heads=8, bring=2, take=2, ahead=8, flops=0, limit=16,
):
    moved = sum(a.size * a.dtype.itemsize for a in args)
    moved += sum(s.size * s.dtype.itemsize for s in outs)
    inside = pl.BlockSpec(memory_space=pltpu.VMEM)
    outside = pl.BlockSpec(memory_space=pltpu.HBM)
    n, m = len(args), len(outs)

    def body(*refs):
        ins, results, scratch = list(refs[:n]), list(refs[n : n + m]), refs[n + m :]
        arrivals, departures = [], []
        for j in range(stream_in):
            arrivals.append(copier(ins[j], scratch[j], scratch[-2], j))
            ins[j] = scratch[j]
        for j in range(stream_out):
            local = scratch[stream_in + j]
            departures.append(copier(local, results[j], scratch[-1], j))
            results[j] = local
        spare = (ins[stream_in], scratch[stream_in + stream_out]) if fetch else None
        io = Stream(
            heads, bring, take, ahead, arrivals, departures, spare, scratch[-3].at[0]
        )
        kernel(io, *ins, *results)
        io.finish()

    streamed = list(args[:stream_in]) + list(outs[:stream_out])
    if fetch:
        streamed.append(args[stream_in])
    args = [
        pltpu.with_memory_space_constraint(a, pltpu.HBM) if j < stream_in + raw else a
        for j, a in enumerate(args)
    ]
    shapes = [pltpu.HBM(s.shape, s.dtype) if j < stream_out else s for j, s in enumerate(outs)]
    return pl.pallas_call(
        body,
        out_shape=tuple(shapes),
        in_specs=[outside] * (stream_in + raw) + [inside] * (n - stream_in - raw),
        out_specs=tuple([outside] * stream_out + [inside] * (m - stream_out)),
        scratch_shapes=[pltpu.VMEM(s.shape, s.dtype) for s in streamed]
        + [
            pltpu.SemaphoreType.DMA((1,)),
            pltpu.SemaphoreType.DMA((max(stream_in, 1), heads // bring)),
            pltpu.SemaphoreType.DMA((max(stream_out, 1), heads // take)),
        ],
        compiler_params=pltpu.CompilerParams(vmem_limit_bytes=limit * MIB),
        cost_estimate=pl.CostEstimate(flops=flops, bytes_accessed=moved, transcendentals=0),
        name=kernel.__name__,
    )(*args)


def shape(dims, dtype=F32):
    return jax.ShapeDtypeStruct(dims, dtype)


def shards(queries, key_rows, value_rows, log_decay, gate_input, out_gain, prior_state, out_grad):
    tokens, features = queries.shape
    heads = log_decay.shape[1]
    count = lax.axis_size("seq")
    peers = lax.axis_size("head")
    groups = count // heads
    near = [[g * heads + m for m in range(heads)] for g in range(groups)]
    far = [[g * heads + m for g in range(groups)] for m in range(heads)]
    wide = (tokens, features)
    states = (heads, HD, HD)
    gain = out_gain[None, :]
    decay = log_decay.T
    product = 2 * tokens * HD * HD * heads

    def exchange(value, axis, members=None):
        return lax.all_to_all(value, axis, 0, 0, axis_index_groups=members)

    parts, remain = call(
        state_kernel,
        [shape((heads, HD + 8, HD)), shape((tokens, heads))],
        key_rows, value_rows, decay,
        stream_in=2, raw=1, fetch=True, stream_out=1, heads=heads, bring=heads, take=4, flops=product,
    )
    parts = exchange(parts, "seq", near)
    within, norm_grad, mixing, scaled, grown, prior = call(
        within_kernel,
        [
            shape(wide), shape(wide), shape((heads, tokens, tokens), BF16),
            shape((heads, HD, tokens), BF16), shape((tokens, heads)), shape((1, HD, HD)),
        ],
        queries, key_rows, value_rows, gate_input, out_grad, prior_state, decay, gain,
        stream_in=5, raw=1, stream_out=4, heads=heads, ahead=2, flops=4 * product, limit=24,
    )
    total, factor = call(
        forward_total_kernel,
        [shape((groups, HD + 8, HD)), shape((heads, 8, HD))],
        within, parts, raw=1,
    )
    total = exchange(total, "seq", far)
    opening, group_factor = call(
        forward_chain_kernel,
        [shape(states), shape((groups, 8, HD))],
        parts, total, factor, prior,
    )
    opening = exchange(opening, "seq", near)
    context, sums = call(
        context_kernel,
        [shape(wide), shape((peers, 2, tokens))],
        queries, within, norm_grad, grown, opening, flops=product,
    )
    sums = exchange(sums, "head")
    parts, inverse, slope = call(
        gradient_kernel,
        [shape(states), shape((tokens, HD)), shape((tokens, HD))],
        scaled, norm_grad, sums, context,
        stream_out=1, heads=heads, take=4, flops=product,
    )
    parts = exchange(parts, "seq", near)
    attended, grad_gate, grad_query, part_k, part_v = call(
        local_backward_kernel,
        [shape(wide, BF16), shape(wide, BF16), shape(wide, BF16), shape(wide), shape(wide)],
        queries, key_rows, value_rows, gate_input, norm_grad, context, mixing, opening,
        decay, grown, gain, inverse, slope,
        stream_in=8, stream_out=5, heads=heads, ahead=2, flops=9 * product, limit=32,
    )
    (total,) = call(
        backward_total_kernel,
        [shape((groups, HD, HD))],
        part_k, parts, factor, raw=1,
    )
    total = exchange(total, "seq", far)
    (returned,) = call(
        backward_chain_kernel, [shape(states)], parts, total, factor, group_factor
    )
    returned = exchange(returned, "seq", near)
    grad_key, grad_value = call(
        finish_kernel,
        [shape(wide, BF16), shape(wide, BF16)],
        key_rows, value_rows, part_k, part_v, returned, remain,
        stream_out=2, heads=heads, flops=2 * product,
    )
    return attended, grad_query, grad_key, grad_value, grad_gate


def solution(mesh):
    wide = P("seq", "head")
    return jax.shard_map(
        shards,
        mesh=mesh,
        in_specs=(wide, wide, wide, wide, wide, P("head"), P("head", None, None), wide),
        out_specs=(wide,) * 5,
        check_vma=False,
    )
```
